32 devices in a mesh: seq: 8 (over z, y), hid: 4 (over x, core).
Axes of the slice: x: 2, y: 2, z: 4, core: 2. Of those that a mesh axis runs over, the one named last changes fastest.
Arguments:
- gate_half: bfloat16 [1024, 2048], P('seq', 'hid'), may hold values from -6 to 6
- value_half: bfloat16 [1024, 2048], P('seq', 'hid'), may hold values from -6 to 6
- norm_gain: float32 [2048], P('hid'), may hold values from 0.25 to 1.75
- norm_shift: float32 [2048], P('hid'), may hold values from -0.5 to 0.5
- token_weight: bfloat16 [1024, 1024], P('seq'), may hold values from -0.25 to 0.25
- token_bias: float32 [1024], P('seq'), may hold values from 0.5 to 1.5
- grad_output: bfloat16 [1024, 2048], P('seq', 'hid'), may hold values from -6 to 6
Outputs:
- grad_gate: bfloat16 [1024, 2048], P('seq', 'hid')
- grad_value: bfloat16 [1024, 2048], P('seq', 'hid')
- grad_gain: float32 [2048], P('hid')
- grad_shift: float32 [2048], P('hid')
- grad_weight: float32 [1024, 1024], P('seq', 'hid')
- grad_token_bias: float32 [1024], P('seq')
The draws below stay inside these ranges and needn't reach their ends.
All inputs are finite; a program needn't handle non-finite values.
Results may differ from the reference program's by a relative error of at most 0.005.
Values may be sent and summed in bfloat16 or wider, within the bound.
No kernel may reach another device: no remote copies, remote signals or barrier semaphores. Data moves between devices by JAX's collectives and lax.ppermute only.
A program may use at most 64 MiB of HBM per device.

```python
import jax
import jax.numpy as jnp
from jax import lax

HIDDEN_SIZE = 2048
TOKENS = 1024


def with_spikes(result, rng, source, target, parts, factor):
    owner, partner = [(jnp.arange(result.shape[axis_at]) // (result.shape[axis_at] // parts)).reshape([-1 if axis == axis_at else 1 for axis in range(result.ndim)]) for axis_at in (source, target)]
    chosen = jax.random.permutation(rng, parts)[partner]
    strong = (owner == chosen) | (owner == (partner + parts // 2) % parts)
    return jnp.where(strong, factor * result, result)


def block_scale(stream_key, dims, cuts, smallest, largest):
    loudness, own = 1.0, jax.random.fold_in(stream_key, 6)
    for position, blocks in cuts:
        steps = jnp.exp(jax.random.uniform(jax.random.fold_in(own, position), (blocks,), jnp.float32, smallest / len(cuts), largest / len(cuts)))
        loudness = loudness * jnp.repeat(steps, dims[position] // blocks).reshape([-1 if axis == position else 1 for axis in range(len(dims))])
    return loudness


def bell_draw(rng, extent, width, reach, cuts=(), kind=jnp.bfloat16):
    result = width * jax.random.normal(rng, extent, jnp.float32)
    if cuts:
        result = result * block_scale(rng, extent, cuts, -0.22, 0.18)
    return jnp.clip(result, -reach, reach).astype(kind)


def bell_draw_with(rng, extent, width, bound, split, heavy, held_as=jnp.bfloat16):
    array = width * jax.random.normal(rng, extent, jnp.float32)
    if split:
        array = array * block_scale(rng, extent, split, -0.22, 0.18)
    return jnp.clip(with_spikes(array, jax.random.fold_in(rng, 3), *heavy), -bound, bound).astype(held_as)


def setup_inputs(seed: int = 0) -> dict:
    arg_keys = jax.random.split(jax.random.key(seed), 8)
    gate_half = bell_draw(arg_keys[0], (TOKENS, HIDDEN_SIZE), 1.0, 6.0, ((0, 8), (1, 4)))
    value_half = bell_draw(arg_keys[1], (TOKENS, HIDDEN_SIZE), 1.0, 6.0, ((0, 8), (1, 4)))
    norm_gain = jnp.clip(1.0 + 0.15 * jax.random.normal(arg_keys[2], (HIDDEN_SIZE,), jnp.float32), 0.25, 1.75)
    norm_shift = jnp.clip(jax.random.uniform(arg_keys[3], (HIDDEN_SIZE,), jnp.float32, -0.5, 0.5) * block_scale(arg_keys[3], (HIDDEN_SIZE,), ((0, 4),), -0.4, 0.0), -0.5, 0.5)
    token_weight = bell_draw_with(arg_keys[4], (TOKENS, TOKENS), TOKENS ** -0.5, 0.25, ((0, 8),), (0, 1, 8, 2.0))
    token_bias = jnp.clip(0.5 + 1.0 * jax.random.uniform(arg_keys[5], (TOKENS,), jnp.float32) ** block_scale(arg_keys[5], (TOKENS,), ((0, 8),), -0.2, 0.2), 0.5, 1.5)
    grad_output = bell_draw(arg_keys[6], (TOKENS, HIDDEN_SIZE), 1.0, 6.0, ((0, 8), (1, 4)))
    return {"gate_half": gate_half, "value_half": value_half, "norm_gain": norm_gain, "norm_shift": norm_shift, "token_weight": token_weight, "token_bias": token_bias, "grad_output": grad_output}


def reference(gate_half, value_half, norm_gain, norm_shift, token_weight, token_bias, grad_output):
    second = value_half.astype(jnp.float32)
    row_mean = lax.optimization_barrier(jnp.sum(second, axis=1, keepdims=True)) / HIDDEN_SIZE
    row_var = lax.optimization_barrier(jnp.sum(second * second, axis=1, keepdims=True)) / HIDDEN_SIZE - row_mean * row_mean
    inv_std = lax.rsqrt(row_var + 1e-05)
    centred = (second - row_mean) * inv_std
    normed = (centred * norm_gain + norm_shift).astype(jnp.bfloat16)
    lower_weight = jnp.tril(token_weight)
    spatial = jnp.dot(lower_weight, normed, preferred_element_type=jnp.float32) + token_bias[:, None]
    upstream = grad_output.astype(jnp.float32)
    grad_gate = (upstream * spatial).astype(jnp.bfloat16)
    grad_mix = (upstream * gate_half.astype(jnp.float32)).astype(jnp.bfloat16)
    grad_weight = jnp.tril(jnp.dot(grad_mix, normed.T, preferred_element_type=jnp.float32))
    grad_token_bias = lax.optimization_barrier(jnp.sum(grad_mix.astype(jnp.float32), axis=1))
    grad_normed = jnp.dot(lower_weight.T, grad_mix, preferred_element_type=jnp.float32)
    grad_gain = lax.optimization_barrier(jnp.sum(grad_normed * centred, axis=0))
    grad_shift = lax.optimization_barrier(jnp.sum(grad_normed, axis=0))
    grad_centred = grad_normed * norm_gain
    first_mean = lax.optimization_barrier(jnp.sum(grad_centred, axis=1, keepdims=True)) / HIDDEN_SIZE
    second_mean = lax.optimization_barrier(jnp.sum(grad_centred * centred, axis=1, keepdims=True)) / HIDDEN_SIZE
    grad_value = (inv_std * (grad_centred - first_mean - centred * second_mean)).astype(jnp.bfloat16)
    return (grad_gate, grad_value, grad_gain, grad_shift, grad_weight, grad_token_bias)
```

```python
import functools

import jax
import jax.numpy as jnp
from jax import lax
from jax.experimental import pallas as pl
from jax.experimental.pallas import tpu as pltpu
from jax.sharding import PartitionSpec as P

HIDDEN_SIZE = 2048
EPS = 1e-05
F32 = jnp.float32
BF16 = jnp.bfloat16


def row_sums(x):
    total = x[:, :128]
    for start in range(128, x.shape[1], 128):
        total = total + x[:, start : start + 128]
    return jnp.sum(total.T, axis=0, keepdims=True)


def split_three(x):
    high = x.astype(BF16)
    rest = x - high.astype(F32)
    middle = rest.astype(BF16)
    low = (rest - middle.astype(F32)).astype(BF16)
    return high, middle, low


def matmul(a, b, contract):
    return lax.dot_general(a, b, (contract, ((), ())), preferred_element_type=F32)


def first_kernel(copies, seq, grad_ref, gate_ref, value_ref, weight_ref, mix_ref, sums_ref, *outgoing):
    rows = value_ref.shape[0]
    me = lax.axis_index("seq")
    mix = (grad_ref[...].astype(F32) * gate_ref[...].astype(F32)).astype(BF16)
    mix_ref[...] = mix
    for step in range(seq - 1, 0, -1):
        other = me ^ step
        out_ref = outgoing[step - 1]

        @pl.when(other < me)
        def _():
            block = weight_ref[:, pl.ds(pl.multiple_of(other * rows, rows), rows)]
            out_ref[...] = matmul(block, mix, ((0,), (0,))).astype(BF16)

        @pl.when(other > me)
        def _():
            out_ref[...] = value_ref[...]

    second = value_ref[...].astype(F32)
    sums = jnp.concatenate(
        [
            row_sums(second),
            row_sums(second * second),
            row_sums(mix.astype(F32)),
            jnp.zeros((5, rows), F32),
        ],
        axis=0,
    )
    for copy in range(copies):
        sums_ref[copy] = sums


def second_kernel(
    seq,
    hid,
    width,
    grad_ref,
    value_ref,
    mix_ref,
    weight_ref,
    gain_ref,
    shift_ref,
    bias_ref,
    sums_ref,
    *refs,
):
    incoming = refs[: seq - 1]
    (
        gate_out_ref,
        normed_grad_ref,
        token_sums_ref,
        stats_ref,
        bias_grad_ref,
        own_outer_ref,
    ) = refs[seq - 1 : seq + 5]
    outgoing = refs[seq + 5 : seq + 4 + hid]
    spatial_ref, outer_ref, total_ref = refs[seq + 4 + hid :]
    rows, channels = value_ref.shape
    me = lax.axis_index("seq")
    me_hid = lax.axis_index("hid")
    gain = gain_ref[...]
    shift = shift_ref[...]
    mix = mix_ref[...]

    def stat_rows(index):
        block = sums_ref[index * hid]
        for part in range(1, hid):
            block = block + sums_ref[index * hid + part]
        return block

    means = []
    inverses = []
    for step in range(seq):
        block = stat_rows(me ^ step)
        mean = block[0:1] / width
        variance = block[1:2] / width - mean * mean
        means.append(mean)
        inverses.append(lax.rsqrt(variance + EPS))
        if step == 0:
            bias_grad_ref[...] = block[2:3]
    mean_columns = jnp.concatenate(means, axis=0)
    inverse_columns = jnp.concatenate(inverses, axis=0)
    stats_ref[...] = jnp.concatenate([means[0], inverses[0], jnp.zeros((6, rows), F32)], axis=0)
    bias_rows = jnp.broadcast_to(bias_ref[...], (8, rows))
    columns = jnp.concatenate([mean_columns, inverse_columns, bias_rows], axis=0).T

    def centre(block, step):
        return (block.astype(F32) - columns[:, step : step + 1]) * columns[:, seq + step : seq + step + 1]

    centred = centre(value_ref[...], 0)
    normed = (centred * gain + shift).astype(BF16)
    lower = lax.broadcasted_iota(jnp.int32, (rows, rows), 1) <= lax.broadcasted_iota(
        jnp.int32, (rows, rows), 0
    )
    here = pl.ds(pl.multiple_of(me * rows, rows), rows)
    diagonal = jnp.where(lower, weight_ref[:, here], jnp.zeros((rows, rows), BF16))
    spatial_ref[...] = matmul(diagonal, normed, ((1,), (0,)))
    outer_ref[:, here] = jnp.where(lower, matmul(mix, normed, ((1,), (1,))), 0.0)
    total_ref[...] = matmul(diagonal, mix, ((0,), (0,)))

    for step in range(1, seq):
        other = me ^ step
        block_ref = incoming[step - 1]
        there = pl.ds(pl.multiple_of(other * rows, rows), rows)

        @pl.when(other < me)
        def _():
            other_normed = (centre(block_ref[...], step) * gain + shift).astype(BF16)
            spatial_ref[...] += matmul(weight_ref[:, there], other_normed, ((1,), (0,)))
            outer_ref[:, there] = matmul(mix, other_normed, ((1,), (1,)))

        @pl.when(other > me)
        def _():
            total_ref[...] += block_ref[...].astype(F32)
            outer_ref[:, there] = jnp.zeros((rows, rows), F32)

    total = total_ref[...]
    normed_grad_ref[...] = total
    grad_centred = total * gain
    channel_sums = jnp.concatenate(
        [row_sums(grad_centred), row_sums(grad_centred * centred), jnp.zeros((6, rows), F32)], axis=0
    )
    own_columns = outer_ref.shape[1] // hid
    for step in range(hid):
        part = pl.ds(pl.multiple_of((me_hid ^ step) * own_columns, own_columns), own_columns)
        if step == 0:
            own_outer_ref[0:rows] = outer_ref[:, part]
            own_outer_ref[rows : rows + 8, 0:rows] = channel_sums
        else:
            out_ref = outgoing[step - 1]
            out_ref[0:rows] = outer_ref[:, part].astype(BF16)
            pieces = jnp.concatenate([x[0:2] for x in split_three(channel_sums)], axis=0)
            out_ref[rows : rows + 16, 0:rows] = jnp.concatenate(
                [pieces, jnp.zeros((10, rows), BF16)], axis=0
            )

    gate_out_ref[...] = (
        grad_ref[...].astype(F32) * (spatial_ref[...] + columns[:, 2 * seq : 2 * seq + 1])
    ).astype(BF16)

    lower_sum = jnp.zeros((rows, 1), F32)
    column_ids = lax.broadcasted_iota(jnp.int32, (rows, weight_ref.shape[1]), 1)
    row_ids = me * rows + lax.broadcasted_iota(jnp.int32, (rows, weight_ref.shape[1]), 0)
    lower_sum = jnp.sum(
        jnp.where(column_ids <= row_ids, weight_ref[...].astype(F32), 0.0), axis=1, keepdims=True
    )
    gain_sum = jnp.sum(total * centred, axis=0, keepdims=True)
    shift_sum = jnp.sum(lower_sum * mix.astype(F32), axis=0, keepdims=True)
    for copy in range(seq):
        token_sums_ref[copy, 0:1] = gain_sum
        token_sums_ref[copy, 1:2] = shift_sum


def third_kernel(
    seq, hid, width, value_ref, normed_grad_ref, gain_ref, stats_ref, own_outer_ref, *refs
):
    incoming = refs[: hid - 1]
    value_out_ref, outer_out_ref = refs[hid - 1 :]
    rows = value_ref.shape[0]
    outer = own_outer_ref[0:rows]
    sums = own_outer_ref[rows : rows + 2, 0:rows]
    for block_ref in incoming:
        outer = outer + block_ref[0:rows].astype(F32)
        pieces = block_ref[rows : rows + 16, 0:rows].astype(F32)
        sums = sums + ((pieces[4:6] + pieces[2:4]) + pieces[0:2])
    outer_out_ref[...] = outer
    columns = jnp.concatenate([stats_ref[...][0:2], sums / width, jnp.zeros((4, rows), F32)], axis=0).T
    inverse = columns[:, 1:2]
    centred = (value_ref[...].astype(F32) - columns[:, 0:1]) * inverse
    grad_centred = normed_grad_ref[...] * gain_ref[...]
    value_out_ref[...] = (
        inverse * (grad_centred - columns[:, 2:3] - centred * columns[:, 3:4])
    ).astype(BF16)


def kernel_call(body, out_shape, scratch_shapes=()):
    return pl.pallas_call(
        body,
        out_shape=out_shape,
        scratch_shapes=scratch_shapes,
    )


def exchange(array, axis, size, step):
    return lax.ppermute(array, axis, [(i, i ^ step) for i in range(size)])


def direct(seq, hid, gate_half, value_half, norm_gain, norm_shift, token_weight, token_bias, grad_output):
    rows, channels = value_half.shape
    tokens = token_weight.shape[1]
    width = channels * hid
    own_columns = tokens // hid
    shape = jax.ShapeDtypeStruct
    block = shape((rows, channels), BF16)
    gain = norm_gain.reshape(1, channels)
    shift = norm_shift.reshape(1, channels)
    mix, sums, *outgoing = kernel_call(
        functools.partial(first_kernel, seq * hid, seq),
        (block, shape((seq * hid, 8, rows), F32)) + (block,) * (seq - 1),
    )(grad_output, gate_half, value_half, token_weight)
    incoming = [None] * (seq - 1)
    for step in range(seq - 1, 0, -1):
        incoming[step - 1] = exchange(outgoing[step - 1], "seq", seq, step)
    all_sums = lax.all_to_all(sums, ("seq", "hid"), 0, 0)
    packed = shape((rows + 16, own_columns), BF16)
    grad_gate, normed_grad, token_sums, stats, grad_token_bias, own_outer, *outgoing = kernel_call(
        functools.partial(second_kernel, seq, hid, width),
        (
            block,
            shape((rows, channels), F32),
            shape((seq, 2, channels), F32),
            shape((8, rows), F32),
            shape((1, rows), F32),
            shape((rows + 8, own_columns), F32),
        )
        + (packed,) * (hid - 1),
        (
            pltpu.VMEM((rows, channels), F32),
            pltpu.VMEM((rows, tokens), F32),
            pltpu.VMEM((rows, channels), F32),
        ),
    )(
        grad_output,
        value_half,
        mix,
        token_weight,
        gain,
        shift,
        token_bias.reshape(1, rows),
        all_sums,
        *incoming,
    )
    incoming = [exchange(outgoing[step - 1], "hid", hid, step) for step in range(1, hid)]
    token_sums = lax.all_to_all(token_sums, "seq", 0, 0)
    token_sums = jnp.sum(token_sums, axis=0)
    grad_value, grad_weight = kernel_call(
        functools.partial(third_kernel, seq, hid, width),
        (block, shape((rows, own_columns), F32)),
    )(value_half, normed_grad, gain, stats, own_outer, *incoming)
    return (
        grad_gate,
        grad_value,
        token_sums[0],
        token_sums[1],
        grad_weight,
        grad_token_bias.reshape(rows),
    )


def gathered(gate_half, value_half, norm_gain, norm_shift, token_weight, token_bias, grad_output):
    local_rows = gate_half.shape[0]
    channels = gate_half.shape[1]
    all_tokens = token_weight.shape[1]
    row_start = lax.axis_index("seq") * local_rows
    row_last = row_start + local_rows - 1
    row_ids = row_start + lax.iota(jnp.int32, local_rows)[:, None]
    second = value_half.astype(jnp.float32)
    upstream = grad_output.astype(jnp.float32)
    grad_mix = (upstream * gate_half.astype(jnp.float32)).astype(jnp.bfloat16)
    sum_first, sum_square, grad_token_bias = lax.psum(
        (
            jnp.sum(second, axis=1),
            jnp.sum(second * second, axis=1),
            jnp.sum(grad_mix.astype(jnp.float32), axis=1),
        ),
        "hid",
    )
    row_mean = (sum_first / HIDDEN_SIZE)[:, None]
    row_var = (sum_square / HIDDEN_SIZE)[:, None] - row_mean * row_mean
    inv_std = lax.rsqrt(row_var + 1e-05)
    centred = (second - row_mean) * inv_std
    normed = (centred * norm_gain + norm_shift).astype(jnp.bfloat16)
    start_pair = (
        jnp.zeros((local_rows, channels), jnp.float32),
        jnp.zeros((local_rows, all_tokens), jnp.float32),
    )
    shard_rows = lax.all_gather(normed, "seq", axis=0, tiled=True)
    length = shard_rows.shape[0]

    def compute(pair):
        weight_block = token_weight
        column_ids = lax.iota(jnp.int32, length)[None, :]
        lower_mask = column_ids <= row_ids
        weight_block = jnp.where(lower_mask, weight_block, jnp.zeros_like(weight_block))
        mixed_sum = jnp.dot(weight_block, shard_rows, preferred_element_type=jnp.float32)
        outer = jnp.einsum("tc,nc->tn", grad_mix, shard_rows, preferred_element_type=jnp.float32)
        outer = jnp.where(lower_mask, outer, 0.0)
        return (mixed_sum, outer)

    mixed_sum, weight_term = lax.cond(
        jnp.int32(0) <= row_last, compute, lambda pair: pair, start_pair
    )
    spatial = mixed_sum + token_bias[:, None]
    grad_gate = (upstream * spatial).astype(jnp.bfloat16)
    grad_weight = lax.psum_scatter(weight_term, "hid", scatter_dimension=1, tiled=True)
    columns = lax.all_to_all(token_weight, "seq", split_axis=1, concat_axis=0, tiled=True)
    own_ids = row_start + lax.iota(jnp.int32, local_rows)[None, :]
    fold_shard_rows = lax.all_gather(grad_mix, "seq", axis=0, tiled=True)
    fold_length = fold_shard_rows.shape[0]

    def compute(running):
        weight_block = columns
        source_ids = lax.iota(jnp.int32, fold_length)[:, None]
        weight_block = jnp.where(source_ids >= own_ids, weight_block, jnp.zeros_like(weight_block))
        return jnp.einsum(
            "nt,nc->tc", weight_block, fold_shard_rows, preferred_element_type=jnp.float32
        )

    grad_normed = lax.cond(
        jnp.int32(0) + fold_length - 1 >= row_start,
        compute,
        lambda running: running,
        jnp.zeros((local_rows, channels), jnp.float32),
    )
    grad_gain, grad_shift = lax.psum(
        (jnp.sum(grad_normed * centred, axis=0), jnp.sum(grad_normed, axis=0)), "seq"
    )
    grad_centred = grad_normed * norm_gain
    sum_grad, sum_cross = lax.psum(
        (jnp.sum(grad_centred, axis=1), jnp.sum(grad_centred * centred, axis=1)), "hid"
    )
    first_mean = (sum_grad / HIDDEN_SIZE)[:, None]
    second_mean = (sum_cross / HIDDEN_SIZE)[:, None]
    grad_value = (inv_std * (grad_centred - first_mean - centred * second_mean)).astype(
        jnp.bfloat16
    )
    return (grad_gate, grad_value, grad_gain, grad_shift, grad_weight, grad_token_bias)


def solution(mesh):
    placed = (
        P("seq", "hid"),
        P("seq", "hid"),
        P("hid"),
        P("hid"),
        P("seq", None),
        P("seq"),
        P("seq", "hid"),
    )
    seq, hid = mesh.shape["seq"], mesh.shape["hid"]

    def per_device(*args):
        rows, tokens = args[4].shape
        small = seq in (2, 4, 8) and hid in (2, 4)
        if small and rows == 128 and args[0].shape[1] % 128 == 0 and (tokens // hid) % 128 == 0:
            return direct(seq, hid, *args)
        return gathered(*args)

    return jax.shard_map(
        per_device,
        mesh=mesh,
        in_specs=placed,
        out_specs=(P("seq", "hid"), P("seq", "hid"), P("hid"), P("hid"), P("seq", "hid"), P("seq")),
        check_vma=False,
    )
```
